256 devices in a mesh: lblk: 32 (over z_hi, x, core), tile: 8 (over y, z_lo).
Axes of the slice: x: 4, y: 4, z: 8 (z_hi: 4, z_lo: 2; z = z_hi * 2 + z_lo), core: 2. Of those that a mesh axis runs over, the one named last changes fastest.
Arguments:
- wavefunction: float32 [4096, 2, 64, 128], P('lblk', None, 'tile'), may hold values from -6 to 6
- l_table: int32 [4096, 2], P('lblk'), may hold values from 0 to 15
- coupling: float32 [32, 8, 128, 128], P('lblk'), may hold values from -2 to 2
- selection: int32 [32, 8], P('lblk'), may hold values 0 or 1
- dipole: float32 [32, 2, 128, 128], P('lblk'), may hold values from -0.5 to 0.5
- field: float32 [1], replicated, may hold values from -0.1 to 0.1
Outputs:
- propagated: float32 [4096, 2, 64, 128], P('lblk', None, 'tile')
The draws below stay inside these ranges and needn't reach their ends.
All inputs are finite; a program needn't handle non-finite values. No bound on the sum of `selection` on one device may be relied on, other than what follows from the above.
Results may differ from the reference program's by a relative error of at most 0.0001.
Values sent between devices are 32-bit elements; how exact they have to be, the bound alone decides.
No kernel may reach another device: no remote copies, remote signals or barrier semaphores. Data moves between devices by JAX's collectives and lax.ppermute only.
A program may use at most 64 MiB of HBM per device.

```python
import jax
import jax.numpy as jnp
from jax import lax

CH = 128
NMP = 8
R2 = 128
TAYLOR = 4
STEPS = 1
NL = 32
NR1 = 64


def draw_wavefunction(key, part):
    key_sign, key_amp = jax.random.split(jax.random.fold_in(key, 11))
    rows = jnp.arange(NR1)
    cols = jnp.arange(R2)
    parity = (1 - 2 * ((rows[:, None] + cols[None, :]) % 2)).astype(jnp.float32)
    part_sign = jnp.where(jax.random.bernoulli(key_sign, 0.5, (1, 2, 1, 1)), 1.0, -1.0).astype(jnp.float32)
    shape = (NL * CH, 2, NR1, R2)
    amplitude = jax.random.uniform(key_amp, shape, jnp.float32, 0.5, 2.5)
    return amplitude * part_sign * parity[None, None]


def draw_coupling(key, part):
    key_sign, key_val = jax.random.split(jax.random.fold_in(key, 23))
    row_sign = jnp.where(jax.random.bernoulli(key_sign, 0.5, (NL, NMP, CH, 1)), 1.0, -1.0).astype(jnp.float32)
    shape = (NL, NMP, CH, CH)
    values = 0.12 + 0.25 * jax.random.normal(key_val, shape, jnp.float32)
    return jnp.clip(row_sign * values, -2.0, 2.0)


def set_ends(values, own_key, least, top_value):
    dims = values.shape
    index_at = [jax.random.randint(jax.random.fold_in(own_key, axis), (), 0, dims[axis]) for axis in range(len(dims))]
    values = values.at[tuple(index_at)].set(least)
    longest = dims.index(max(dims))
    index_at[longest] = (index_at[longest] + 1) % dims[longest]
    return values.at[tuple(index_at)].set(top_value)


def block_scale(rng, shape, cuts, smallest, largest):
    def one(axis_at, blocks):
        heights = jax.random.uniform(jax.random.fold_in(jax.random.fold_in(rng, 6), axis_at), (blocks,), jnp.float32, smallest / len(cuts), largest / len(cuts))
        return jnp.repeat(jnp.exp(heights), shape[axis_at] // blocks).reshape((-1,) + (1,) * (len(shape) - axis_at - 1))

    loudness = one(*cuts[0])
    for cut in cuts[1:]:
        loudness = loudness * one(*cut)
    return loudness


def centred(rng, shape, width, bound, shards=(), dtype=jnp.bfloat16):
    array = width * jax.random.normal(rng, shape, jnp.float32)
    if shards:
        array = array * block_scale(rng, shape, shards, -0.22, 0.18)
    return jnp.clip(array, -bound, bound).astype(dtype)


def setup_inputs(seed: int = 0) -> dict:
    keys = jax.random.split(jax.random.key(seed), 7)
    return {
        "wavefunction": draw_wavefunction(jax.random.fold_in(keys[6], 71), 0),
        "l_table": set_ends(jax.random.randint(keys[1], (NL * CH, 2), 0, 16), jax.random.fold_in(keys[1], 1), 0, 15).astype(jnp.int32),
        "coupling": draw_coupling(jax.random.fold_in(keys[6], 71), 0),
        "selection": set_ends((jax.random.randint(keys[3], (NL, NMP), 0, 4) < 3).astype(jnp.int32), jax.random.fold_in(keys[3], 1), 0, 1),
        "dipole": centred(keys[4], (NL, 2, CH, CH), CH ** -0.5, 0.5, ((0, 32),), jnp.float32),
        "field": jnp.clip(jax.random.uniform(keys[5], (STEPS,), jnp.float32, -0.1, 0.1), -0.1, 0.1),
    }


time_step = 0.03
grid_step = 0.5
radius_start = 8.0


def second_diff(padded, along, length_along):
    def window(offset):
        return lax.slice_in_dim(padded, offset, offset + length_along, axis=along)
    return (-window(0) + 16.0 * window(1) - 30.0 * window(2) + 16.0 * window(3) - window(4)) / (12.0 * grid_step * grid_step)


def mat_product(matrix, field_in):
    flat = field_in.reshape(field_in.shape[0], -1)
    out = jnp.dot(matrix, flat, precision=lax.Precision.HIGHEST, preferred_element_type=jnp.float32)
    return out.reshape(field_in.shape)


def reference(wavefunction, l_table, coupling, selection, dipole, field):
    row_count = wavefunction.shape[2]
    col_count = wavefunction.shape[3]
    channels = CH
    radius_one = radius_start + grid_step * jnp.arange(row_count).astype(jnp.float32)
    radius_two = radius_start + grid_step * jnp.arange(col_count).astype(jnp.float32)
    larger = jnp.maximum(radius_one[:, None], radius_two[None, :])
    smaller = jnp.minimum(radius_one[:, None], radius_two[None, :])
    orders = jnp.arange(NMP).astype(jnp.float32)
    radial = (smaller / larger)[None] ** orders[:, None, None] / larger[None]
    weights = 0.5 * (coupling + jnp.swapaxes(coupling, 2, 3)) * selection.astype(jnp.float32)[:, :, None, None]
    angular = l_table.astype(jnp.float32).reshape(NL, channels, 2)
    base_pot = -2.0 / radius_one[:, None] - 2.0 / radius_two[None, :]
    dip_low = jnp.pad(dipole, ((1, 0), (0, 0), (0, 0), (0, 0)))[:-1]
    scale_one = radius_one[None, None, :, None]
    scale_two = radius_two[None, None, None, :]

    def hamiltonian(series_term, strength):
        blocks = series_term.reshape(NL, channels, 2, row_count, col_count)
        padded_l = jnp.pad(blocks, ((1, 1), (0, 0), (0, 0), (0, 0), (0, 0)))
        block_above = padded_l[2:]
        block_below = padded_l[:-2]

        def one_block(items):
            field_in, upper_in, lower_in, weight_blk, coupling_up, coupling_down, ang = items
            pad_one = jnp.pad(field_in, ((0, 0), (0, 0), (2, 2), (0, 0)))
            pad_two = jnp.pad(field_in, ((0, 0), (0, 0), (0, 0), (2, 2)))
            laplace_sum = second_diff(pad_one, 2, row_count) + second_diff(pad_two, 3, col_count)
            cent = (ang[:, 0] * (ang[:, 0] + 1.0) / 2.0)[:, None, None] / (radius_one[None, :, None] ** 2) + (ang[:, 1] * (ang[:, 1] + 1.0) / 2.0)[:, None, None] / (radius_two[None, None, :] ** 2)
            potential = base_pot[None] + cent
            result = -0.5 * laplace_sum + potential[:, None] * field_in
            for multi in range(NMP):
                result = result + mat_product(weight_blk[multi], radial[multi][None, None] * field_in)
            dipole_term = mat_product(coupling_up[0], scale_one * upper_in) + mat_product(coupling_up[1], scale_two * upper_in)
            dipole_term = dipole_term + mat_product(coupling_down[0].T, scale_one * lower_in) + mat_product(coupling_down[1].T, scale_two * lower_in)
            return result + strength * dipole_term

        applied = lax.map(one_block, (blocks, block_above, block_below, weights, dipole, dip_low, angular))
        return applied.reshape(series_term.shape)

    total = wavefunction
    for step_index in range(STEPS):
        strength = field[step_index]
        series_term = total
        accum = total
        for order_index in range(1, TAYLOR + 1):
            applied = hamiltonian(series_term, strength)
            series_term = (time_step / order_index) * jnp.stack([applied[:, 1], -applied[:, 0]], axis=1)
            accum = accum + series_term
        total = accum
    return total
```

```python
import functools

import jax
import jax.numpy as jnp
from jax import lax
from jax.experimental import pallas as pl
from jax.experimental.pallas import tpu as pltpu
from jax.sharding import PartitionSpec as P

NMP = 8
TAYLOR = 4

time_step = 0.03
grid_step = 0.5
radius_start = 8.0

NEAR = -0.5 * 16.0 / (12.0 * grid_step * grid_step)
FAR = 0.5 * 1.0 / (12.0 * grid_step * grid_step)
CENTRE = 2.0 * 0.5 * 30.0 / (12.0 * grid_step * grid_step)

F32 = jnp.float32
BF16 = jnp.bfloat16


def params(limit=40 << 20):
    return pltpu.CompilerParams(dimension_semantics=None, vmem_limit_bytes=limit)


def cost(flops, moved):
    return pl.CostEstimate(flops=flops, bytes_accessed=moved, transcendentals=0)


def whole(shape):
    zeros = (0,) * len(shape)
    return pl.BlockSpec(shape, lambda *_: zeros)


def row_spec():
    return pl.BlockSpec((1, 2, 128, 128), lambda i: (i, 0, 0, 0))


SCALAR = pl.BlockSpec(memory_space=pltpu.SMEM)


def split(value):
    high = value.astype(BF16)
    return high, (value - high.astype(F32)).astype(BF16)


def row_radius(i):
    row = lax.axis_index("tile") * 8 + i
    return radius_start + grid_step * row.astype(F32)


def col_radius(shape):
    col = lax.broadcasted_iota(jnp.int32, shape, len(shape) - 1) % 128
    return radius_start + grid_step * col.astype(F32)


def natural(ref, i, part):
    return ref[pl.ds(part * 8 + i, 128, stride=16), :]


def both(ref, i, first, row):
    if first:
        return jnp.concatenate([natural(ref, i, 0), natural(ref, i, 1)], axis=1)
    return jnp.concatenate([ref[row, 0], ref[row, 1]], axis=1)


def operand(value):
    high, low = split(value)
    return jnp.concatenate([high, low, high], axis=0)


def stacked(matrix):
    high, low = split(matrix)
    return jnp.concatenate([high, high, low], axis=1)


def edges_kernel(psi_ref, h1_ref, h2_ref):
    even = lax.rem(lax.axis_index("tile"), 2) == 0

    def store(ref, start):
        for row in range(2):
            for part in range(2):
                ref[row, part] = natural(psi_ref, start + row, part)

    store(h1_ref, jnp.where(even, 6, 0))
    store(h2_ref, jnp.where(even, 0, 6))


def weights_kernel(sel_ref, coup_ref, l_ref, wcat_ref, radial_ref, ang_ref):
    for k in range(NMP):
        matrix = coup_ref[0, k]
        matrix = 0.5 * (matrix + matrix.T) * sel_ref[0, k].astype(F32)
        wcat_ref[pl.ds(k * 128, 128), :] = stacked(matrix)
    offset = lax.axis_index("tile") * 8
    rows = lax.broadcasted_iota(jnp.int32, (8, 256), 0) + offset
    one = radius_start + grid_step * rows.astype(F32)
    two = col_radius((8, 256))
    larger = jnp.maximum(one, two)
    ratio = jnp.minimum(one, two) / larger
    term = 1.0 / larger
    for k in range(NMP):
        radial_ref[k] = term
        if k < NMP - 1:
            term = term * ratio
    for e in range(2):
        ang = l_ref[:, e : e + 1].astype(F32)
        ang_ref[e] = jnp.broadcast_to(ang * (ang + 1.0) / 2.0, (128, 128))


def dipole_kernel(field_ref, own_ref, below_ref, d1_ref, d2_ref):
    even = lax.rem(lax.axis_index("lblk"), 2) == 0
    strength = field_ref[0]
    for e in range(2):
        up = stacked(own_ref[0, e] * strength)
        down = stacked(below_ref[0, e].T * strength)
        rows = pl.ds(e * 128, 128)

        @pl.when(even)
        def _():
            d1_ref[rows, :] = up
            d2_ref[rows, :] = down

        @pl.when(jnp.logical_not(even))
        def _():
            d1_ref[rows, :] = down
            d2_ref[rows, :] = up


def dipole_part(i, d_ref, other):
    out = jnp.dot(d_ref[...], operand(other), preferred_element_type=F32)
    return row_radius(i) * out[:128] + col_radius((1, 256)) * out[128:]


def local_kernel(first, step, w_ref, other_ref, psi_ref, wcat_ref, d_ref, radial_ref, ang_ref, q_ref):
    i = pl.program_id(0)
    mine = both(w_ref, i, first, i)
    prod = jnp.dot(wcat_ref[...], operand(mine), preferred_element_type=F32)
    total = dipole_part(i, d_ref, both(other_ref, i, first, 0))
    for k in range(NMP):
        total = total + radial_ref[k, pl.ds(i, 1), :] * prod[k * 128 : (k + 1) * 128]
    for shift in (-2, -1, 1, 2):
        place = i + shift
        inside = jnp.logical_and(place >= 0, place < 8)
        weight = jnp.where(inside, NEAR if abs(shift) == 1 else FAR, 0.0)
        place = jnp.clip(place, 0, 7)
        total = total + weight * both(w_ref, place, first, place)
    one = row_radius(i)
    two = col_radius((1, 128))
    lane = lax.broadcasted_iota(jnp.int32, (1, 128), 1)
    potential = (
        ang_ref[0] * (1.0 / (one * one))
        + ang_ref[1] * (1.0 / (two * two))
        + (CENTRE - 2.0 / one - 2.0 / two)
    )
    half = []
    for part in range(2):
        value = mine[:, part * 128 : (part + 1) * 128]
        near = jnp.where(lane >= 1, pltpu.roll(value, 1, 1), 0.0) + jnp.where(
            lane < 127, pltpu.roll(value, 127, 1), 0.0
        )
        far = jnp.where(lane >= 2, pltpu.roll(value, 2, 1), 0.0) + jnp.where(
            lane < 126, pltpu.roll(value, 126, 1), 0.0
        )
        half.append(
            total[:, part * 128 : (part + 1) * 128] + potential * value + NEAR * near + FAR * far
        )
    q_ref[0, 0] = natural(psi_ref, i, 0) + step * half[1]
    q_ref[0, 1] = natural(psi_ref, i, 1) - step * half[0]


def finish_kernel(first, last, step, q_ref, other_ref, h1_ref, h2_ref, d_ref, *refs):
    if last:
        out_ref, g_ref = refs
    else:
        out_ref, s1_ref, s2_ref, g_ref = refs
    i = pl.program_id(0)
    even = lax.rem(lax.axis_index("tile"), 2) == 0
    g_ref[...] = dipole_part(i, d_ref, both(other_ref, i, first, 0))
    low = i < 2
    high = i >= 6
    zero = jnp.float32(0.0)
    c0 = jnp.where(low, jnp.where(i == 0, FAR, zero), jnp.where(i == 6, FAR, NEAR))
    c1 = jnp.where(low, jnp.where(i == 0, NEAR, FAR), jnp.where(i == 6, zero, FAR))
    use1 = jnp.logical_or(jnp.logical_and(low, ~even), jnp.logical_and(high, even))
    use2 = jnp.logical_or(jnp.logical_and(low, even), jnp.logical_and(high, ~even))

    def halo(ref):
        for part in range(2):
            cols = pl.ds(part * 128, 128)
            g_ref[:, cols] += c0 * ref[0, part] + c1 * ref[1, part]

    @pl.when(use1)
    def _():
        halo(h1_ref)

    @pl.when(use2)
    def _():
        halo(h2_ref)

    real = q_ref[0, 0] + step * g_ref[:, 128:]
    imag = q_ref[0, 1] - step * g_ref[:, :128]
    if last:
        out_ref[pl.ds(i, 128, stride=16), :] = real
        out_ref[pl.ds(8 + i, 128, stride=16), :] = imag
        return
    out_ref[0, 0] = real
    out_ref[0, 1] = imag
    slot = jnp.where(low, i, i - 6)

    @pl.when(use1)
    def _():
        s1_ref[slot, 0] = real
        s1_ref[slot, 1] = imag

    @pl.when(use2)
    def _():
        s2_ref[slot, 0] = real
        s2_ref[slot, 1] = imag


FIELD = (8, 2, 128, 128)
EDGE = (2, 2, 128, 128)
FLAT = (2048, 128)


def shape(dims, dtype=F32):
    return jax.ShapeDtypeStruct(dims, dtype)


def local_call(first, step, w, other, psi, wcat, d, radial, ang):
    return pl.pallas_call(
        functools.partial(local_kernel, first, step),
        grid=(8,),
        in_specs=[
            whole(FLAT if first else FIELD),
            whole(FLAT) if first else row_spec(),
            whole(FLAT),
            whole((1024, 384)),
            whole((256, 384)),
            whole((8, 8, 256)),
            whole((2, 128, 128)),
        ],
        out_specs=row_spec(),
        out_shape=shape(FIELD),
        compiler_params=params(),
        cost_estimate=cost(2 * 2048 * 1280 * 384, 6 << 20),
        name="local",
    )(w, other, psi, wcat, d, radial, ang)


def finish_call(first, last, step, q, other, h1, h2, d):
    return pl.pallas_call(
        functools.partial(finish_kernel, first, last, step),
        grid=(8,),
        in_specs=[
            row_spec(),
            whole(FLAT) if first else row_spec(),
            whole(EDGE),
            whole(EDGE),
            whole((256, 384)),
        ],
        out_specs=[whole(FLAT)] if last else [row_spec(), whole(EDGE), whole(EDGE)],
        out_shape=[shape(FLAT)] if last else [shape(FIELD), shape(EDGE), shape(EDGE)],
        scratch_shapes=[pltpu.VMEM((128, 256), F32)],
        compiler_params=params(),
        cost_estimate=cost(2 * 2048 * 256 * 384, 4 << 20),
        name="finish",
    )(q, other, h1, h2, d)


def swaps(count, start):
    pairs = []
    for low in range(start, count - 1, 2):
        pairs += [(low, low + 1), (low + 1, low)]
    return pairs


def per_device(wavefunction, l_table, coupling, selection, dipole, field):
    blocks, tiles = lax.axis_size("lblk"), lax.axis_size("tile")
    psi = wavefunction.reshape(FLAT)
    inner = lambda value: lax.ppermute(value, "lblk", swaps(blocks, 0))
    outer = lambda value: lax.ppermute(value, "lblk", swaps(blocks, 1))
    edge1 = lambda value: lax.ppermute(value, "tile", swaps(tiles, 0))
    edge2 = lambda value: lax.ppermute(value, "tile", swaps(tiles, 1))

    below = lax.ppermute(dipole, "lblk", [(k, k + 1) for k in range(blocks - 1)])
    s1, s2 = pl.pallas_call(
        edges_kernel,
        in_specs=[whole(FLAT)],
        out_specs=[whole(EDGE)] * 2,
        out_shape=[shape(EDGE)] * 2,
        grid=(1,),
        compiler_params=params(),
        cost_estimate=cost(0, 2 << 20),
        name="edges",
    )(psi)
    wcat, radial, ang = pl.pallas_call(
        weights_kernel,
        grid=(1,),
        in_specs=[SCALAR, whole((1, 8, 128, 128)), whole((128, 2))],
        out_specs=[whole((1024, 384)), whole((8, 8, 256)), whole((2, 128, 128))],
        out_shape=[shape((1024, 384), BF16), shape((8, 8, 256)), shape((2, 128, 128))],
        compiler_params=params(),
        cost_estimate=cost(1 << 20, 2 << 20),
        name="weights",
    )(selection, coupling, l_table)
    d1, d2 = pl.pallas_call(
        dipole_kernel,
        grid=(1,),
        in_specs=[SCALAR, whole((1, 2, 128, 128)), whole((1, 2, 128, 128))],
        out_specs=[whole((256, 384))] * 2,
        out_shape=[shape((256, 384), BF16)] * 2,
        compiler_params=params(),
        cost_estimate=cost(1 << 20, 1 << 20),
        name="dipole",
    )(field, dipole, below)

    w = psi
    for order in range(TAYLOR, 0, -1):
        first, last = order == TAYLOR, order == 1
        step = time_step / order
        far = outer(w)
        h2 = edge2(s2)
        h1 = edge1(s1)
        near = inner(w)
        q = local_call(first, step, w, near, psi, wcat, d1, radial, ang)
        got = finish_call(first, last, step, q, far, h1, h2, d2)
        if last:
            return got[0].reshape(wavefunction.shape)
        w, s1, s2 = got


def solution(mesh):
    placed = (
        P("lblk", None, "tile", None),
        P("lblk", None),
        P("lblk", None, None, None),
        P("lblk", None),
        P("lblk", None, None, None),
        P(),
    )
    return jax.shard_map(
        per_device,
        mesh=mesh,
        in_specs=placed,
        out_specs=P("lblk", None, "tile", None),
        check_vma=False,
    )
```

```python
import functools

import jax
import jax.numpy as jnp
from jax import lax
from jax.experimental import pallas as pl
from jax.experimental.pallas import tpu as pltpu
from jax.sharding import PartitionSpec as P


NMP = 8
TAYLOR = 4
STRAIGHT = 5

time_step = 0.03
grid_step = 0.5
radius_start = 8.0

NEAR = -0.5 * 16.0 / (12.0 * grid_step * grid_step)
FAR = 0.5 * 1.0 / (12.0 * grid_step * grid_step)
CENTRE = 2.0 * 0.5 * 30.0 / (12.0 * grid_step * grid_step)

F32 = jnp.float32
BF16 = jnp.bfloat16


def params(limit=40 << 20):
    return pltpu.CompilerParams(dimension_semantics=None, vmem_limit_bytes=limit)


def cost(flops, moved):
    return pl.CostEstimate(flops=flops, bytes_accessed=moved, transcendentals=0)


def whole(shape):
    zeros = (0,) * len(shape)
    return pl.BlockSpec(shape, lambda *_: zeros)


def row_spec():
    return pl.BlockSpec((1, 2, 128, 128), lambda i: (i, 0, 0, 0))


SCALAR = pl.BlockSpec(memory_space=pltpu.SMEM)


def split(value):
    high = value.astype(BF16)
    return high, (value - high.astype(F32)).astype(BF16)


def row_radius(i):
    row = lax.axis_index("tile") * 8 + i
    return radius_start + grid_step * row.astype(F32)


def col_radius(shape):
    col = lax.broadcasted_iota(jnp.int32, shape, len(shape) - 1) % 128
    return radius_start + grid_step * col.astype(F32)


def natural(ref, i, part, count=128):
    return ref[pl.ds(part * 8 + i, count, stride=16), :]


def both(ref, row):
    return jnp.concatenate([ref[row, 0], ref[row, 1]], axis=1)


def operand(value):
    high, low = split(value)
    return jnp.concatenate([high, low, high], axis=0)


def stacked(matrix):
    high, low = split(matrix)
    return jnp.concatenate([high, high, low], axis=1)


def unpack_kernel(psi_ref, w_ref, fa_ref, fb_ref, s1_ref, s2_ref):
    even = lax.rem(lax.axis_index("tile"), 2) == 0
    for row in range(8):
        for part in range(2):
            value = natural(psi_ref, row, part)
            w_ref[row, part] = value
            if row < STRAIGHT:
                fa_ref[row, part] = value
            else:
                fb_ref[row - STRAIGHT, part] = value
    for row in range(2):
        for part in range(2):
            low, high = w_ref[row, part], w_ref[6 + row, part]
            s1_ref[row, part] = jnp.where(even, high, low)
            s2_ref[row, part] = jnp.where(even, low, high)


def weights_kernel(sel_ref, coup_ref, l_ref, wcat_ref, radial_ref, ang_ref):
    for k in range(NMP):
        matrix = coup_ref[0, k]
        matrix = 0.5 * (matrix + matrix.T) * sel_ref[0, k].astype(F32)
        wcat_ref[pl.ds(k * 128, 128), :] = stacked(matrix)
    offset = lax.axis_index("tile") * 8
    rows = lax.broadcasted_iota(jnp.int32, (8, 256), 0) + offset
    one = radius_start + grid_step * rows.astype(F32)
    two = col_radius((8, 256))
    larger = jnp.maximum(one, two)
    ratio = jnp.minimum(one, two) / larger
    term = 1.0 / larger
    for k in range(NMP):
        radial_ref[k] = term
        if k < NMP - 1:
            term = term * ratio
    for e in range(2):
        ang = l_ref[:, e : e + 1].astype(F32)
        ang_ref[e] = jnp.broadcast_to(ang * (ang + 1.0) / 2.0, (128, 128))


def dipole_kernel(field_ref, own_ref, below_ref, d1_ref, d2_ref):
    even = lax.rem(lax.axis_index("lblk"), 2) == 0
    strength = field_ref[0]
    for e in range(2):
        up = stacked(own_ref[0, e] * strength)
        down = stacked(below_ref[0, e].T * strength)
        rows = pl.ds(e * 128, 128)

        @pl.when(even)
        def _():
            d1_ref[rows, :] = up
            d2_ref[rows, :] = down

        @pl.when(jnp.logical_not(even))
        def _():
            d1_ref[rows, :] = down
            d2_ref[rows, :] = up


def dipole_part(i, d_ref, other):
    out = jnp.dot(d_ref[...], operand(other), preferred_element_type=F32)
    return row_radius(i) * out[:128] + col_radius((1, 256)) * out[128:]


def local_kernel(step, w_ref, other_ref, psi_ref, wcat_ref, d_ref, radial_ref, ang_ref, q_ref):
    i = pl.program_id(0)
    mine = both(w_ref, i)
    prod = jnp.dot(wcat_ref[...], operand(mine), preferred_element_type=F32)
    total = dipole_part(i, d_ref, both(other_ref, 0))
    for k in range(NMP):
        total = total + radial_ref[k, pl.ds(i, 1), :] * prod[k * 128 : (k + 1) * 128]
    for shift in (-2, -1, 1, 2):
        place = i + shift
        inside = jnp.logical_and(place >= 0, place < 8)
        weight = jnp.where(inside, NEAR if abs(shift) == 1 else FAR, 0.0)
        place = jnp.clip(place, 0, 7)
        total = total + weight * both(w_ref, place)
    one = row_radius(i)
    two = col_radius((1, 128))
    lane = lax.broadcasted_iota(jnp.int32, (1, 128), 1)
    potential = (
        ang_ref[0] * (1.0 / (one * one))
        + ang_ref[1] * (1.0 / (two * two))
        + (CENTRE - 2.0 / one - 2.0 / two)
    )
    half = []
    for part in range(2):
        value = mine[:, part * 128 : (part + 1) * 128]
        near = jnp.where(lane >= 1, pltpu.roll(value, 1, 1), 0.0) + jnp.where(
            lane < 127, pltpu.roll(value, 127, 1), 0.0
        )
        far = jnp.where(lane >= 2, pltpu.roll(value, 2, 1), 0.0) + jnp.where(
            lane < 126, pltpu.roll(value, 126, 1), 0.0
        )
        half.append(
            total[:, part * 128 : (part + 1) * 128] + potential * value + NEAR * near + FAR * far
        )
    q_ref[0, 0] = natural(psi_ref, i, 0) + step * half[1]
    q_ref[0, 1] = natural(psi_ref, i, 1) - step * half[0]


def far_row(i, ra_ref, rb_ref, rc_ref):
    place = lax.rem(lax.axis_index("lblk"), 8)
    relayed = jnp.logical_or(place == 0, place == 7)
    parts = [
        jnp.where(
            i < STRAIGHT, ra_ref[0, part], jnp.where(relayed, rc_ref[0, part], rb_ref[0, part])
        )
        for part in range(2)
    ]
    return jnp.concatenate(parts, axis=1)


def finish_kernel(last, step, q_ref, ra_ref, rb_ref, rc_ref, h1_ref, h2_ref, d_ref, *refs):
    if last:
        out_ref, g_ref = refs
    else:
        out_ref, fa_ref, fb_ref, s1_ref, s2_ref, g_ref = refs
    i = pl.program_id(0)
    even = lax.rem(lax.axis_index("tile"), 2) == 0
    g_ref[...] = dipole_part(i, d_ref, far_row(i, ra_ref, rb_ref, rc_ref))
    low = i < 2
    high = i >= 6
    zero = jnp.float32(0.0)
    c0 = jnp.where(low, jnp.where(i == 0, FAR, zero), jnp.where(i == 6, FAR, NEAR))
    c1 = jnp.where(low, jnp.where(i == 0, NEAR, FAR), jnp.where(i == 6, zero, FAR))
    use1 = jnp.logical_or(jnp.logical_and(low, ~even), jnp.logical_and(high, even))
    use2 = jnp.logical_or(jnp.logical_and(low, even), jnp.logical_and(high, ~even))

    def halo(ref):
        for part in range(2):
            cols = pl.ds(part * 128, 128)
            g_ref[:, cols] += c0 * ref[0, part] + c1 * ref[1, part]

    @pl.when(use1)
    def _():
        halo(h1_ref)

    @pl.when(use2)
    def _():
        halo(h2_ref)

    real = q_ref[0, 0] + step * g_ref[:, 128:]
    imag = q_ref[0, 1] - step * g_ref[:, :128]
    if last:
        out_ref[pl.ds(i, 128, stride=16), :] = real
        out_ref[pl.ds(8 + i, 128, stride=16), :] = imag
        return

    def store(ref, row):
        ref[row, 0] = real
        ref[row, 1] = imag

    slot = jnp.where(low, i, i - 6)
    store(out_ref, 0)
    pl.when(i < STRAIGHT)(lambda: store(fa_ref, 0))
    pl.when(i >= STRAIGHT)(lambda: store(fb_ref, 0))
    pl.when(use1)(lambda: store(s1_ref, slot))
    pl.when(use2)(lambda: store(s2_ref, slot))


FIELD = (8, 2, 128, 128)
EDGE = (2, 2, 128, 128)
FLAT = (2048, 128)
EARLY = (STRAIGHT, 2, 128, 128)
LATE = (8 - STRAIGHT, 2, 128, 128)


def shape(dims, dtype=F32):
    return jax.ShapeDtypeStruct(dims, dtype)


def local_call(step, w, other, psi, wcat, d, radial, ang):
    return pl.pallas_call(
        functools.partial(local_kernel, step),
        grid=(8,),
        in_specs=[
            whole(FIELD),
            row_spec(),
            whole(FLAT),
            whole((1024, 384)),
            whole((256, 384)),
            whole((8, 8, 256)),
            whole((2, 128, 128)),
        ],
        out_specs=row_spec(),
        out_shape=shape(FIELD),
        compiler_params=params(),
        cost_estimate=cost(2 * 2048 * 1280 * 384, 6 << 20),
        name="local",
    )(w, other, psi, wcat, d, radial, ang)


def early_rows():
    return pl.BlockSpec((1, 2, 128, 128), lambda i: (jnp.minimum(i, STRAIGHT - 1), 0, 0, 0))


def late_rows():
    return pl.BlockSpec((1, 2, 128, 128), lambda i: (jnp.maximum(i - STRAIGHT, 0), 0, 0, 0))


SENT = [FIELD, EARLY, LATE, EDGE, EDGE]


def finish_call(last, step, q, ra, rb, rc, h1, h2, d):
    return pl.pallas_call(
        functools.partial(finish_kernel, last, step),
        grid=(8,),
        in_specs=[
            row_spec(),
            early_rows(),
            late_rows(),
            late_rows(),
            whole(EDGE),
            whole(EDGE),
            whole((256, 384)),
        ],
        out_specs=[whole(FLAT)]
        if last
        else [row_spec(), early_rows(), late_rows(), whole(EDGE), whole(EDGE)],
        out_shape=[shape(dims) for dims in ([FLAT] if last else SENT)],
        scratch_shapes=[pltpu.VMEM((128, 256), F32)],
        compiler_params=params(),
        cost_estimate=cost(2 * 2048 * 256 * 384, 4 << 20),
        name="finish",
    )(q, ra, rb, rc, h1, h2, d)


def swaps(count, start):
    pairs = []
    for low in range(start, count - 1, 2):
        pairs += [(low, low + 1), (low + 1, low)]
    return pairs


def relay_pairs(blocks):
    pairs = []
    for low in range(1, blocks - 1, 2):
        if low % 8 == 7:
            pairs += [(low, low - 7), (low + 1, low + 8)]
        else:
            pairs += [(low, low + 1), (low + 1, low)]
    onward = []
    for low in range(7, blocks - 1, 8):
        onward += [(low - 7, low + 1), (low + 8, low)]
    return pairs, onward


def per_device(wavefunction, l_table, coupling, selection, dipole, field):
    blocks, tiles = lax.axis_size("lblk"), lax.axis_size("tile")
    psi = wavefunction.reshape(FLAT)
    relay, onward = relay_pairs(blocks)

    below = lax.ppermute(dipole, "lblk", [(k, k + 1) for k in range(blocks - 1)])
    w, fa, fb, s1, s2 = pl.pallas_call(
        unpack_kernel,
        in_specs=[whole(FLAT)],
        out_specs=[whole(dims) for dims in SENT],
        out_shape=[shape(dims) for dims in SENT],
        grid=(1,),
        compiler_params=params(),
        cost_estimate=cost(0, 4 << 20),
        name="unpack",
    )(psi)
    wcat, radial, ang = pl.pallas_call(
        weights_kernel,
        grid=(1,),
        in_specs=[SCALAR, whole((1, 8, 128, 128)), whole((128, 2))],
        out_specs=[whole((1024, 384)), whole((8, 8, 256)), whole((2, 128, 128))],
        out_shape=[shape((1024, 384), BF16), shape((8, 8, 256)), shape((2, 128, 128))],
        compiler_params=params(),
        cost_estimate=cost(1 << 20, 2 << 20),
        name="weights",
    )(selection, coupling, l_table)
    d1, d2 = pl.pallas_call(
        dipole_kernel,
        grid=(1,),
        in_specs=[SCALAR, whole((1, 2, 128, 128)), whole((1, 2, 128, 128))],
        out_specs=[whole((256, 384))] * 2,
        out_shape=[shape((256, 384), BF16)] * 2,
        compiler_params=params(),
        cost_estimate=cost(1 << 20, 1 << 20),
        name="dipole",
    )(field, dipole, below)

    for order in range(TAYLOR, 0, -1):
        last = order == 1
        step = time_step / order
        ra = lax.ppermute(fa, "lblk", swaps(blocks, 1))
        rb = lax.ppermute(fb, "lblk", relay)
        h2 = lax.ppermute(s2, "tile", swaps(tiles, 1))
        h1 = lax.ppermute(s1, "tile", swaps(tiles, 0))
        near = lax.ppermute(w, "lblk", swaps(blocks, 0))
        rc = lax.ppermute(rb, "lblk", onward)
        q = local_call(step, w, near, psi, wcat, d1, radial, ang)
        got = finish_call(last, step, q, ra, rb, rc, h1, h2, d2)
        if last:
            return got[0].reshape(wavefunction.shape)
        w, fa, fb, s1, s2 = got


def solution(mesh):
    placed = (
        P("lblk", None, "tile", None),
        P("lblk", None),
        P("lblk", None, None, None),
        P("lblk", None),
        P("lblk", None, None, None),
        P(),
    )
    return jax.shard_map(
        per_device,
        mesh=mesh,
        in_specs=placed,
        out_specs=P("lblk", None, "tile", None),
        check_vma=False,
    )
```

```python
import functools

import jax
import jax.numpy as jnp
from jax import lax
from jax.experimental import pallas as pl
from jax.experimental.pallas import tpu as pltpu
from jax.sharding import PartitionSpec as P


NMP = 8
TAYLOR = 4
STRAIGHT = 5

time_step = 0.03
grid_step = 0.5
radius_start = 8.0

NEAR = -0.5 * 16.0 / (12.0 * grid_step * grid_step)
FAR = 0.5 * 1.0 / (12.0 * grid_step * grid_step)
CENTRE = 2.0 * 0.5 * 30.0 / (12.0 * grid_step * grid_step)

F32 = jnp.float32
BF16 = jnp.bfloat16


def params(limit=40 << 20):
    return pltpu.CompilerParams(dimension_semantics=None, vmem_limit_bytes=limit)


def cost(flops, moved):
    return pl.CostEstimate(flops=flops, bytes_accessed=moved, transcendentals=0)


def whole(shape):
    zeros = (0,) * len(shape)
    return pl.BlockSpec(shape, lambda *_: zeros)


VMEM = pl.BlockSpec(memory_space=pltpu.VMEM)


SCALAR = pl.BlockSpec(memory_space=pltpu.SMEM)


def split(value):
    high = value.astype(BF16)
    return high, (value - high.astype(F32)).astype(BF16)


def row_radius(i):
    row = lax.axis_index("tile") * 8 + jnp.int32(i)
    return radius_start + grid_step * row.astype(F32)


def col_radius(shape):
    col = lax.broadcasted_iota(jnp.int32, shape, len(shape) - 1) % 128
    return radius_start + grid_step * col.astype(F32)


def natural(ref, i, part, count=128):
    return ref[pl.ds(part * 8 + i, count, stride=16), :]


def both(ref, row):
    return jnp.concatenate([ref[row, 0], ref[row, 1]], axis=1)


def operand(value):
    high, low = split(value)
    return jnp.concatenate([high, low, high], axis=0)


def stacked(matrix):
    high, low = split(matrix)
    return jnp.concatenate([high, high, low], axis=1)


def unpack_kernel(psi_ref, w_ref, fa_ref, fb_ref, s1_ref, s2_ref):
    even = lax.rem(lax.axis_index("tile"), 2) == 0
    for row in range(8):
        for part in range(2):
            value = natural(psi_ref, row, part)
            w_ref[row, part] = value
            if row < STRAIGHT:
                fa_ref[row, part] = value
            else:
                fb_ref[row - STRAIGHT, part] = value
    for row in range(2):
        for part in range(2):
            low, high = w_ref[row, part], w_ref[6 + row, part]
            s1_ref[row, part] = jnp.where(even, high, low)
            s2_ref[row, part] = jnp.where(even, low, high)


def weights_kernel(sel_ref, coup_ref, l_ref, wcat_ref, radial_ref, ang_ref):
    for k in range(NMP):
        matrix = coup_ref[0, k]
        matrix = 0.5 * (matrix + matrix.T) * sel_ref[0, k].astype(F32)
        wcat_ref[pl.ds(k * 128, 128), :] = stacked(matrix)
    offset = lax.axis_index("tile") * 8
    rows = lax.broadcasted_iota(jnp.int32, (8, 256), 0) + offset
    one = radius_start + grid_step * rows.astype(F32)
    two = col_radius((8, 256))
    larger = jnp.maximum(one, two)
    ratio = jnp.minimum(one, two) / larger
    term = 1.0 / larger
    for k in range(NMP):
        radial_ref[k] = term
        if k < NMP - 1:
            term = term * ratio
    for e in range(2):
        ang = l_ref[:, e : e + 1].astype(F32)
        ang_ref[e] = jnp.broadcast_to(ang * (ang + 1.0) / 2.0, (128, 128))


def dipole_kernel(field_ref, own_ref, below_ref, d1_ref, d2_ref):
    even = lax.rem(lax.axis_index("lblk"), 2) == 0
    strength = field_ref[0]
    for e in range(2):
        up = stacked(own_ref[0, e] * strength)
        down = stacked(below_ref[0, e].T * strength)
        rows = pl.ds(e * 128, 128)

        @pl.when(even)
        def _():
            d1_ref[rows, :] = up
            d2_ref[rows, :] = down

        @pl.when(jnp.logical_not(even))
        def _():
            d1_ref[rows, :] = down
            d2_ref[rows, :] = up


def dipole_part(i, d_ref, other):
    out = jnp.dot(d_ref[...], operand(other), preferred_element_type=F32)
    return row_radius(i) * out[:128] + col_radius((1, 256)) * out[128:]


def local_kernel(step, w_ref, other_ref, psi_ref, wcat_ref, d_ref, radial_ref, ang_ref, q_ref):
    def row(i, carry):
        mine = both(w_ref, i)
        prod = jnp.dot(wcat_ref[...], operand(mine), preferred_element_type=F32)
        total = dipole_part(i, d_ref, both(other_ref, i))
        for k in range(NMP):
            total = total + radial_ref[k, pl.ds(i, 1), :] * prod[k * 128 : (k + 1) * 128]
        for shift in (-2, -1, 1, 2):
            place = i + shift
            inside = jnp.logical_and(place >= 0, place < 8)
            weight = jnp.where(inside, NEAR if abs(shift) == 1 else FAR, 0.0)
            place = jnp.clip(place, 0, 7)
            total = total + weight * both(w_ref, place)
        one = row_radius(i)
        two = col_radius((1, 128))
        lane = lax.broadcasted_iota(jnp.int32, (1, 128), 1)
        potential = (
            ang_ref[0] * (1.0 / (one * one))
            + ang_ref[1] * (1.0 / (two * two))
            + (CENTRE - 2.0 / one - 2.0 / two)
        )
        half = []
        for part in range(2):
            value = mine[:, part * 128 : (part + 1) * 128]
            near = jnp.where(lane >= 1, pltpu.roll(value, 1, 1), 0.0) + jnp.where(
                lane < 127, pltpu.roll(value, 127, 1), 0.0
            )
            far = jnp.where(lane >= 2, pltpu.roll(value, 2, 1), 0.0) + jnp.where(
                lane < 126, pltpu.roll(value, 126, 1), 0.0
            )
            half.append(
                total[:, part * 128 : (part + 1) * 128]
                + potential * value
                + NEAR * near
                + FAR * far
            )
        q_ref[i, 0] = natural(psi_ref, i, 0) + step * half[1]
        q_ref[i, 1] = natural(psi_ref, i, 1) - step * half[0]
        return carry

    lax.fori_loop(0, 8, row, 0)


def finish_kernel(last, step, q_ref, ra_ref, rb_ref, rc_ref, h1_ref, h2_ref, d_ref, *refs):
    place = lax.rem(lax.axis_index("lblk"), 8)
    relayed = jnp.logical_or(place == 0, place == 7)
    even = lax.rem(lax.axis_index("tile"), 2) == 0
    for i in range(8):
        if i < STRAIGHT:
            other = both(ra_ref, i)
        else:
            late = i - STRAIGHT
            other = jnp.where(relayed, both(rc_ref, late), both(rb_ref, late))
        total = dipole_part(i, d_ref, other)
        if i < 2 or i >= 6:
            weights = {0: (FAR, NEAR), 1: (None, FAR), 6: (FAR, None), 7: (NEAR, FAR)}[i]
            for row, weight in enumerate(weights):
                if weight is not None:
                    one, two = both(h1_ref, row), both(h2_ref, row)
                    total = total + weight * (
                        jnp.where(even, two, one) if i < 2 else jnp.where(even, one, two)
                    )
        real = q_ref[i, 0] + step * total[:, 128:]
        imag = q_ref[i, 1] - step * total[:, :128]
        if last:
            refs[0][pl.ds(i, 128, stride=16), :] = real
            refs[0][pl.ds(8 + i, 128, stride=16), :] = imag
            continue
        w_ref, fa_ref, fb_ref, s1_ref, s2_ref = refs

        def store(ref, row):
            ref[row, 0] = real
            ref[row, 1] = imag

        store(w_ref, i)
        if i < STRAIGHT:
            store(fa_ref, i)
        else:
            store(fb_ref, i - STRAIGHT)
        if i < 2:
            pl.when(even)(functools.partial(store, s2_ref, i))
            pl.when(jnp.logical_not(even))(functools.partial(store, s1_ref, i))
        if i >= 6:
            pl.when(even)(functools.partial(store, s1_ref, i - 6))
            pl.when(jnp.logical_not(even))(functools.partial(store, s2_ref, i - 6))


FIELD = (8, 2, 128, 128)
EDGE = (2, 2, 128, 128)
FLAT = (2048, 128)
EARLY = (STRAIGHT, 2, 128, 128)
LATE = (8 - STRAIGHT, 2, 128, 128)


def shape(dims, dtype=F32):
    return jax.ShapeDtypeStruct(dims, dtype)


def call(kernel, inputs, outputs, flops, moved, limit=40 << 20):
    return pl.pallas_call(
        kernel,
        in_specs=[SCALAR if small else VMEM for _, small in inputs],
        out_specs=[VMEM] * len(outputs),
        out_shape=[shape(*o) if isinstance(o[0], tuple) else shape(o) for o in outputs],
        compiler_params=params(limit),
        cost_estimate=cost(flops, moved),
    )(*[value for value, _ in inputs])


def local_call(step, *operands):
    (q,) = call(
        functools.partial(local_kernel, step),
        [(value, False) for value in operands],
        [FIELD],
        2 * 2048 * 1280 * 384,
        6 << 20,
    )
    return q


SENT = [FIELD, EARLY, LATE, EDGE, EDGE]


def finish_call(last, step, *operands):
    return call(
        functools.partial(finish_kernel, last, step),
        [(value, False) for value in operands],
        [FLAT] if last else SENT,
        2 * 2048 * 256 * 384,
        4 << 20,
    )


def swaps(count, start):
    pairs = []
    for low in range(start, count - 1, 2):
        pairs += [(low, low + 1), (low + 1, low)]
    return pairs


def relay_pairs(blocks):
    pairs = []
    for low in range(1, blocks - 1, 2):
        if low % 8 == 7:
            pairs += [(low, low - 7), (low + 1, low + 8)]
        else:
            pairs += [(low, low + 1), (low + 1, low)]
    onward = []
    for low in range(7, blocks - 1, 8):
        onward += [(low - 7, low + 1), (low + 8, low)]
    return pairs, onward


def per_device(wavefunction, l_table, coupling, selection, dipole, field):
    blocks, tiles = lax.axis_size("lblk"), lax.axis_size("tile")
    psi = wavefunction.reshape(FLAT)
    relay, onward = relay_pairs(blocks)

    below = lax.ppermute(dipole, "lblk", [(k, k + 1) for k in range(blocks - 1)])
    w, fa, fb, s1, s2 = pl.pallas_call(
        unpack_kernel,
        in_specs=[whole(FLAT)],
        out_specs=[whole(dims) for dims in SENT],
        out_shape=[shape(dims) for dims in SENT],
        grid=(1,),
        compiler_params=params(),
        cost_estimate=cost(0, 4 << 20),
        name="unpack",
    )(psi)
    wcat, radial, ang = pl.pallas_call(
        weights_kernel,
        grid=(1,),
        in_specs=[SCALAR, whole((1, 8, 128, 128)), whole((128, 2))],
        out_specs=[whole((1024, 384)), whole((8, 8, 256)), whole((2, 128, 128))],
        out_shape=[shape((1024, 384), BF16), shape((8, 8, 256)), shape((2, 128, 128))],
        compiler_params=params(),
        cost_estimate=cost(1 << 20, 2 << 20),
        name="weights",
    )(selection, coupling, l_table)
    d1, d2 = pl.pallas_call(
        dipole_kernel,
        grid=(1,),
        in_specs=[SCALAR, whole((1, 2, 128, 128)), whole((1, 2, 128, 128))],
        out_specs=[whole((256, 384))] * 2,
        out_shape=[shape((256, 384), BF16)] * 2,
        compiler_params=params(),
        cost_estimate=cost(1 << 20, 1 << 20),
        name="dipole",
    )(field, dipole, below)

    for order in range(TAYLOR, 0, -1):
        last = order == 1
        step = time_step / order
        ra = lax.ppermute(fa, "lblk", swaps(blocks, 1))
        rb = lax.ppermute(fb, "lblk", relay)
        h2 = lax.ppermute(s2, "tile", swaps(tiles, 1))
        h1 = lax.ppermute(s1, "tile", swaps(tiles, 0))
        near = lax.ppermute(w, "lblk", swaps(blocks, 0))
        rc = lax.ppermute(rb, "lblk", onward)
        q = local_call(step, w, near, psi, wcat, d1, radial, ang)
        got = finish_call(last, step, q, ra, rb, rc, h1, h2, d2)
        if last:
            return got[0].reshape(wavefunction.shape)
        w, fa, fb, s1, s2 = got


def solution(mesh):
    placed = (
        P("lblk", None, "tile", None),
        P("lblk", None),
        P("lblk", None, None, None),
        P("lblk", None),
        P("lblk", None, None, None),
        P(),
    )
    return jax.shard_map(
        per_device,
        mesh=mesh,
        in_specs=placed,
        out_specs=P("lblk", None, "tile", None),
        check_vma=False,
    )
```

```python
import functools
import itertools

import jax
import jax.numpy as jnp
from jax import lax
from jax.experimental import pallas as pl
from jax.experimental.pallas import tpu as pltpu
from jax.sharding import PartitionSpec as P


NMP = 8
TAYLOR = 4
STRAIGHT = 5

time_step = 0.03
grid_step = 0.5
radius_start = 8.0

NEAR = -0.5 * 16.0 / (12.0 * grid_step * grid_step)
FAR = 0.5 * 1.0 / (12.0 * grid_step * grid_step)
CENTRE = 2.0 * 0.5 * 30.0 / (12.0 * grid_step * grid_step)

F32 = jnp.float32
BF16 = jnp.bfloat16


def params(limit=16 << 20):
    return pltpu.CompilerParams(dimension_semantics=None, vmem_limit_bytes=limit)


def cost(flops, moved):
    return pl.CostEstimate(flops=flops, bytes_accessed=moved, transcendentals=0)


def whole(shape):
    zeros = (0,) * len(shape)
    return pl.BlockSpec(shape, lambda *_: zeros)


VMEM = pl.BlockSpec(memory_space=pltpu.VMEM)


SCALAR = pl.BlockSpec(memory_space=pltpu.SMEM)


def split(value):
    high = value.astype(BF16)
    return high, (value - high.astype(F32)).astype(BF16)


def actual(i):
    odd = lax.rem(lax.axis_index("tile"), 2)
    return jnp.int32(i) + odd * (7 - 2 * jnp.int32(i))


def row_radius(i):
    row = lax.axis_index("tile") * 8 + actual(i)
    return radius_start + grid_step * row.astype(F32)


def col_radius(shape):
    col = lax.broadcasted_iota(jnp.int32, shape, len(shape) - 1) % 128
    return radius_start + grid_step * col.astype(F32)


def natural(ref, i, part):
    return ref[pl.ds(part * 8 + actual(i), 128, stride=16), :]


def both(ref, row):
    return jnp.concatenate([ref[row, 0], ref[row, 1]], axis=1)


def operand(value):
    high, low = split(value)
    return jnp.concatenate([high, low, high], axis=0)


def stacked(matrix):
    high, low = split(matrix)
    return jnp.concatenate([high, high, low], axis=1)


def unpack_kernel(psi_ref, w_ref, fa_ref, fb_ref, s1_ref, s2_ref):
    for row in range(8):
        for part in range(2):
            value = natural(psi_ref, row, part)
            w_ref[row, part] = value
            if row < STRAIGHT:
                fa_ref[row, part] = value
            else:
                fb_ref[row - STRAIGHT, part] = value
            if row < 2:
                s2_ref[row, part] = value
            if row >= 6:
                s1_ref[row - 6, part] = value


def weights_kernel(sel_ref, coup_ref, l_ref, wcat_ref, radial_ref, ang_ref):
    for k in range(NMP):
        matrix = coup_ref[0, k]
        matrix = 0.5 * (matrix + matrix.T) * sel_ref[0, k].astype(F32)
        wcat_ref[pl.ds(k * 128, 128), :] = stacked(matrix)
    offset = lax.axis_index("tile") * 8
    rows = lax.broadcasted_iota(jnp.int32, (8, 256), 0)
    rows = rows + lax.rem(lax.axis_index("tile"), 2) * (7 - 2 * rows) + offset
    one = radius_start + grid_step * rows.astype(F32)
    two = col_radius((8, 256))
    larger = jnp.maximum(one, two)
    ratio = jnp.minimum(one, two) / larger
    term = 1.0 / larger
    for k in range(NMP):
        radial_ref[k] = term
        if k < NMP - 1:
            term = term * ratio
    for e in range(2):
        ang = l_ref[:, e : e + 1].astype(F32)
        ang_ref[e] = jnp.broadcast_to(ang * (ang + 1.0) / 2.0, (128, 128))


def dipole_kernel(field_ref, own_ref, below_ref, d1_ref, d2_ref):
    even = lax.rem(lax.axis_index("lblk"), 2) == 0
    strength = field_ref[0]
    for e in range(2):
        up = stacked(own_ref[0, e] * strength)
        down = stacked(below_ref[0, e].T * strength)
        rows = pl.ds(e * 128, 128)

        @pl.when(even)
        def _():
            d1_ref[rows, :] = up
            d2_ref[rows, :] = down

        @pl.when(jnp.logical_not(even))
        def _():
            d1_ref[rows, :] = down
            d2_ref[rows, :] = up


def dipole_part(i, d_ref, other):
    out = jnp.dot(d_ref[...], operand(other), preferred_element_type=F32)
    return row_radius(i) * out[:128] + col_radius((1, 256)) * out[128:]


def local_kernel(step, w_ref, other_ref, psi_ref, wcat_ref, d_ref, radial_ref, ang_ref, q_ref):
    def row(i, carry):
        mine = both(w_ref, i)
        prod = jnp.dot(wcat_ref[...], operand(mine), preferred_element_type=F32)
        total = dipole_part(i, d_ref, both(other_ref, i))
        for k in range(NMP):
            total = total + radial_ref[k, pl.ds(i, 1), :] * prod[k * 128 : (k + 1) * 128]
        for shift in (-2, -1, 1, 2):
            place = i + shift
            inside = jnp.logical_and(place >= 0, place < 8)
            weight = jnp.where(inside, NEAR if abs(shift) == 1 else FAR, 0.0)
            place = jnp.clip(place, 0, 7)
            total = total + weight * both(w_ref, place)
        one = row_radius(i)
        two = col_radius((1, 128))
        lane = lax.broadcasted_iota(jnp.int32, (1, 128), 1)
        potential = (
            ang_ref[0] * (1.0 / (one * one))
            + ang_ref[1] * (1.0 / (two * two))
            + (CENTRE - 2.0 / one - 2.0 / two)
        )
        half = []
        for part in range(2):
            value = mine[:, part * 128 : (part + 1) * 128]
            near = jnp.where(lane >= 1, pltpu.roll(value, 1, 1), 0.0) + jnp.where(
                lane < 127, pltpu.roll(value, 127, 1), 0.0
            )
            far = jnp.where(lane >= 2, pltpu.roll(value, 2, 1), 0.0) + jnp.where(
                lane < 126, pltpu.roll(value, 126, 1), 0.0
            )
            half.append(
                total[:, part * 128 : (part + 1) * 128]
                + potential * value
                + NEAR * near
                + FAR * far
            )
        q_ref[i, 0] = natural(psi_ref, i, 0) + step * half[1]
        q_ref[i, 1] = natural(psi_ref, i, 1) - step * half[0]
        return carry

    lax.fori_loop(0, 8, row, 0)


def finished(step, q_ref, d_ref, i, other, edge):
    total = dipole_part(i, d_ref, other)
    for row, weight in edge.items():
        total = total + weight * row()
    return q_ref[i, 0] + step * total[:, 128:], q_ref[i, 1] - step * total[:, :128]


def late_rows(step, q_ref, rb_ref, rc_ref, h1_ref, d_ref):
    place = lax.rem(lax.axis_index("lblk"), 8)
    relayed = jnp.logical_or(place == 0, place == 7)
    for i in range(STRAIGHT, 8):
        late = i - STRAIGHT
        other = jnp.where(relayed, both(rc_ref, late), both(rb_ref, late))
        edge = {}
        if i == 6:
            edge = {lambda: both(h1_ref, 1): FAR}
        if i == 7:
            edge = {lambda: both(h1_ref, 1): NEAR, lambda: both(h1_ref, 0): FAR}
        yield i, finished(step, q_ref, d_ref, i, other, edge)


def early_rows(step, q_ref, ra_ref, h2_ref, d_ref):
    for i in range(STRAIGHT):
        edge = {}
        if i == 1:
            edge = {lambda: both(h2_ref, 0): FAR}
        if i == 0:
            edge = {lambda: both(h2_ref, 0): NEAR, lambda: both(h2_ref, 1): FAR}
        yield i, finished(step, q_ref, d_ref, i, both(ra_ref, i), edge)


def finish_late_kernel(step, q_ref, rb_ref, rc_ref, h1_ref, d_ref, fb_ref, s1_ref):
    for i, values in late_rows(step, q_ref, rb_ref, rc_ref, h1_ref, d_ref):
        for part, value in enumerate(values):
            fb_ref[i - STRAIGHT, part] = value
            if i >= 6:
                s1_ref[i - 6, part] = value


def finish_early_kernel(step, q_ref, ra_ref, h2_ref, d_ref, fb_ref, w_ref, fa_ref, s2_ref):
    for i, values in early_rows(step, q_ref, ra_ref, h2_ref, d_ref):
        for part, value in enumerate(values):
            w_ref[i, part] = value
            fa_ref[i, part] = value
            if i < 2:
                s2_ref[i, part] = value
    for i in range(STRAIGHT, 8):
        w_ref[i] = fb_ref[i - STRAIGHT]


def finish_last_kernel(
    step, q_ref, ra_ref, rb_ref, rc_ref, h1_ref, h2_ref, d_ref, out_ref
):
    early = early_rows(step, q_ref, ra_ref, h2_ref, d_ref)
    late = late_rows(step, q_ref, rb_ref, rc_ref, h1_ref, d_ref)
    for i, values in itertools.chain(early, late):
        for part, value in enumerate(values):
            out_ref[pl.ds(part * 8 + actual(i), 128, stride=16), :] = value


FIELD = (8, 2, 128, 128)
EDGE = (2, 2, 128, 128)
FLAT = (2048, 128)
EARLY = (STRAIGHT, 2, 128, 128)
LATE = (8 - STRAIGHT, 2, 128, 128)


def shape(dims, dtype=F32):
    return jax.ShapeDtypeStruct(dims, dtype)


def call(kernel, inputs, outputs, flops, moved, limit=16 << 20):
    return pl.pallas_call(
        kernel,
        in_specs=[SCALAR if small else VMEM for _, small in inputs],
        out_specs=[VMEM] * len(outputs),
        out_shape=[shape(*o) if isinstance(o[0], tuple) else shape(o) for o in outputs],
        compiler_params=params(limit),
        cost_estimate=cost(flops, moved),
    )(*[value for value, _ in inputs])


def local_call(step, *operands):
    (q,) = call(
        functools.partial(local_kernel, step),
        [(value, False) for value in operands],
        [FIELD],
        2 * 2048 * 1280 * 384,
        6 << 20,
    )
    return q


SENT = [FIELD, EARLY, LATE, EDGE, EDGE]


def finish_call(kernel, step, outputs, rows, *operands):
    return call(
        functools.partial(kernel, step),
        [(value, False) for value in operands],
        outputs,
        2 * rows * 256 * 256 * 384,
        rows << 19,
    )


def swaps(count, start):
    pairs = []
    for low in range(start, count - 1, 2):
        pairs += [(low, low + 1), (low + 1, low)]
    return pairs


def relay_pairs(blocks):
    pairs = []
    for low in range(1, blocks - 1, 2):
        if low % 8 == 7:
            pairs += [(low, low - 7), (low + 1, low + 8)]
        else:
            pairs += [(low, low + 1), (low + 1, low)]
    onward = []
    for low in range(7, blocks - 1, 8):
        onward += [(low - 7, low + 1), (low + 8, low)]
    return pairs, onward


def per_device(wavefunction, l_table, coupling, selection, dipole, field):
    blocks, tiles = lax.axis_size("lblk"), lax.axis_size("tile")
    psi = wavefunction.reshape(FLAT)
    relay, onward = relay_pairs(blocks)

    below = lax.ppermute(dipole, "lblk", [(k, k + 1) for k in range(blocks - 1)])
    w, fa, fb, s1, s2 = pl.pallas_call(
        unpack_kernel,
        in_specs=[whole(FLAT)],
        out_specs=[whole(dims) for dims in SENT],
        out_shape=[shape(dims) for dims in SENT],
        grid=(1,),
        compiler_params=params(),
        cost_estimate=cost(0, 4 << 20),
        name="unpack",
    )(psi)
    wcat, radial, ang = pl.pallas_call(
        weights_kernel,
        grid=(1,),
        in_specs=[SCALAR, whole((1, 8, 128, 128)), whole((128, 2))],
        out_specs=[whole((1024, 384)), whole((8, 8, 256)), whole((2, 128, 128))],
        out_shape=[shape((1024, 384), BF16), shape((8, 8, 256)), shape((2, 128, 128))],
        compiler_params=params(),
        cost_estimate=cost(1 << 20, 2 << 20),
        name="weights",
    )(selection, coupling, l_table)
    d1, d2 = pl.pallas_call(
        dipole_kernel,
        grid=(1,),
        in_specs=[SCALAR, whole((1, 2, 128, 128)), whole((1, 2, 128, 128))],
        out_specs=[whole((256, 384))] * 2,
        out_shape=[shape((256, 384), BF16)] * 2,
        compiler_params=params(),
        cost_estimate=cost(1 << 20, 1 << 20),
        name="dipole",
    )(field, dipole, below)

    for n in range(TAYLOR):
        step = time_step / (TAYLOR - n)
        rb = lax.ppermute(fb, "lblk", relay)
        h1 = lax.ppermute(s1, "tile", swaps(tiles, 0))
        ra = lax.ppermute(fa, "lblk", swaps(blocks, 1))
        h2 = lax.ppermute(s2, "tile", swaps(tiles, 1))
        near = lax.ppermute(w, "lblk", swaps(blocks, 0))
        rc = lax.ppermute(rb, "lblk", onward)
        q = local_call(step, w, near, psi, wcat, d1, radial, ang)
        if n == TAYLOR - 1:
            (out,) = finish_call(finish_last_kernel, step, [FLAT], 8, q, ra, rb, rc, h1, h2, d2)
            return out.reshape(wavefunction.shape)
        fb, s1 = finish_call(finish_late_kernel, step, [LATE, EDGE], 3, q, rb, rc, h1, d2)
        w, fa, s2 = finish_call(
            finish_early_kernel, step, [FIELD, EARLY, EDGE], 5, q, ra, h2, d2, fb
        )


def solution(mesh):
    placed = (
        P("lblk", None, "tile", None),
        P("lblk", None),
        P("lblk", None, None, None),
        P("lblk", None),
        P("lblk", None, None, None),
        P(),
    )
    return jax.shard_map(
        per_device,
        mesh=mesh,
        in_specs=placed,
        out_specs=P("lblk", None, "tile", None),
        check_vma=False,
    )
```
